32 devices in a mesh: dp: 8 (over z, y), tensor: 4 (over x, core).
Axes of the slice: x: 2, y: 2, z: 4, core: 2. Of those that a mesh axis runs over, the one named last changes fastest.
Arguments:
- tokens: bfloat16 [8, 2048, 768], P('dp', 'tensor'), may hold values from -6 to 6
- cotangent: bfloat16 [8, 2048, 768], P('dp', 'tensor'), may hold values from -8 to 8
- seg_ids: int32 [8, 2048], P('dp'), may hold values from 0 to 7, never falling along the last dimension, each value on 1 to 1024 neighbouring positions
- mix_weight: bfloat16 [768, 2304], P(('dp', 'tensor')), may hold values from -0.21875 to 0.21875
- out_weight: bfloat16 [768, 768], P(('dp', 'tensor')), may hold values from -0.875 to 0.875
- gate_weight: bfloat16 [768, 3072], P('dp', 'tensor'), may hold values from -0.21875 to 0.21875
- up_weight: bfloat16 [768, 3072], P('dp', 'tensor'), may hold values from -0.21875 to 0.21875
- down_weight: bfloat16 [3072, 768], P('tensor', 'dp'), may hold values from -0.109375 to 0.109375
- first_gain: bfloat16 [768], P(('dp', 'tensor')), may hold values from 0.25 to 1.75
- first_shift: bfloat16 [768], P(('dp', 'tensor')), may hold values from -1.75 to 1.75
- second_gain: bfloat16 [768], P(('dp', 'tensor')), may hold values from 0.25 to 1.75
- second_shift: bfloat16 [768], P(('dp', 'tensor')), may hold values from -1.75 to 1.75
Outputs:
- output: float32 [8, 2048, 768], P('dp', 'tensor')
- grad_tokens: float32 [8, 2048, 768], P('dp', 'tensor')
- grad_mix: float32 [768, 2304], P(('dp', 'tensor'))
- grad_out: float32 [768, 768], P(('dp', 'tensor'))
- grad_gate: float32 [768, 3072], P('dp', 'tensor')
- grad_up: float32 [768, 3072], P('dp', 'tensor')
- grad_down: float32 [3072, 768], P('tensor', 'dp')
- grad_first_gain: float32 [768], P(('dp', 'tensor'))
- grad_first_shift: float32 [768], P(('dp', 'tensor'))
- grad_second_gain: float32 [768], P(('dp', 'tensor'))
- grad_second_shift: float32 [768], P(('dp', 'tensor'))
The draws below stay inside these ranges and needn't reach their ends.
Inputs may be any that keep to these rules, and one draw needn't show every extreme that they name: `seg_ids`: along each row ids never fall; each id is one document of 1 to 1024 consecutive tokens, and some document has exactly 1024 tokens.
All inputs are finite; a program needn't handle non-finite values.
Results may differ from the reference program's by a relative error of at most 0.019.
Values may be sent and summed in bfloat16 or wider, within the bound.
A program may use at most 320 MiB of HBM per device.

```python
import math
import jax
import jax.numpy as jnp
import numpy as np
from jax import lax

D = 768
HEAD_DIM = 64
FF = 3072
SEQ = 2048
SEGS = 8
MAXDOC = 1024
ROWS = 8


def strengthened(values, rng, source, target, blocks, factor):
    owner, partner = [(jnp.arange(values.shape[dim]) // (values.shape[dim] // blocks)).reshape([-1 if axis == dim else 1 for axis in range(values.ndim)]) for dim in (source, target)]
    chosen = jax.random.permutation(rng, blocks)[partner]
    strong = (owner == chosen) | (owner == (partner + blocks // 2) % blocks)
    return jnp.where(strong, factor * values, values)


def steps_of(stream_key, extent, cuts, least, top_value):
    def one(position, blocks):
        steps = jax.random.uniform(jax.random.fold_in(jax.random.fold_in(stream_key, 6), position), (blocks,), jnp.float32, least / len(cuts), top_value / len(cuts))
        return jnp.repeat(jnp.exp(steps), extent[position] // blocks).reshape((-1,) + (1,) * (len(extent) - position - 1))

    level = one(*cuts[0])
    for cut in cuts[1:]:
        level = level * one(*cut)
    return level


def split_up(count, total, limit, skew):
    portions = [(1 << 20) // math.isqrt(standing ** skew) + 1 for standing in range(2, count + 1)]
    surplus, holding = total - limit - (count - 1), [1] * (count - 1)
    while surplus > 0:
        movable = [i for i in range(count - 1) if holding[i] < limit]
        whole, left = sum([portions[i] for i in movable]), surplus
        for i in movable:
            more = min(limit - holding[i], max(1, left * portions[i] // whole), surplus)
            holding[i] = holding[i] + more
            surplus = surplus - more
    return np.array([limit] + holding)


def ragged(rng, number_of, total, reach, skew):
    if number_of == 2:
        one = jax.random.randint(rng, (), max(1, total - reach), min(reach, total - 1) + 1)
        return jnp.stack([one, total - one])
    lengths = jnp.asarray(split_up(number_of, total, reach, skew), jnp.int32)
    couples = (number_of - 1) // 2
    giver, receiver = lengths[1:1 + 2 * couples:2], lengths[2:2 + 2 * couples:2]
    slack = jnp.minimum(giver - 1, reach - receiver)
    moved = jax.random.randint(jax.random.fold_in(rng, 1), (couples,), 0, 1 << 20) % (slack + 1)
    lengths = lengths.at[1:1 + 2 * couples:2].set(giver - moved).at[2:2 + 2 * couples:2].set(receiver + moved)
    return lengths[jax.random.permutation(jax.random.fold_in(rng, 2), number_of)]


def centred(own_key, shape, scale, reach, cuts=(), held_as=jnp.bfloat16):
    values = jax.random.normal(own_key, shape, jnp.float32) * scale
    if len(cuts) > 0:
        values = steps_of(own_key, shape, cuts, -0.22, 0.18) * values
    return jnp.clip(values, min=-reach, max=reach).astype(held_as)


def bell_draw_with(key, extent, spread, most, cuts, heavy, held_as=jnp.bfloat16):
    array = spread * jax.random.normal(key, extent, jnp.float32)
    if cuts:
        array = array * steps_of(key, extent, cuts, -0.22, 0.18)
    return jnp.clip(strengthened(array, jax.random.fold_in(key, 3), *heavy), -most, most).astype(held_as)


def setup_inputs(seed: int = 0) -> dict:
    keys = jax.random.split(jax.random.key(seed), 13)
    tokens = centred(keys[0], (ROWS, SEQ, D), 1.0, 6.0, ((0, 8), (1, 4)))
    cotangent = bell_draw_with(keys[1], (ROWS, SEQ, D), 1.0, 8.0, ((0, 8), (1, 4)), (0, 2, 8, 2.0))
    seg_ids = jax.vmap(lambda own: jnp.searchsorted(jnp.cumsum(ragged(own, SEGS, SEQ, MAXDOC, 2)), jnp.arange(SEQ), side="right"))(jax.random.split(keys[2], ROWS)).reshape((ROWS, SEQ)).astype(jnp.int32)
    mix_weight = centred(keys[3], (D, 3 * D), D ** -0.5, 0.21875, ((0, 32),))
    out_weight = centred(keys[4], (D, D), (D // 16) ** -0.5, 0.875, ((0, 32),))
    gate_weight = centred(keys[5], (D, FF), D ** -0.5, 0.21875, ((0, 8), (1, 4)))
    up_weight = centred(keys[6], (D, FF), D ** -0.5, 0.21875, ((0, 8), (1, 4)))
    down_weight = centred(keys[7], (FF, D), FF ** -0.5, 0.109375, ((0, 4), (1, 8)))
    first_gain = jnp.clip(1.0 + 0.15 * jax.random.normal(keys[8], (D,), jnp.float32), 0.25, 1.75).astype(jnp.bfloat16)
    first_shift = centred(keys[9], (D,), 0.3, 1.75, ((0, 32),))
    second_gain = jnp.clip(1.0 + 0.15 * jax.random.normal(keys[10], (D,), jnp.float32), 0.25, 1.75).astype(jnp.bfloat16)
    second_shift = centred(keys[11], (D,), 0.3, 1.75, ((0, 32),))
    return dict(tokens=tokens, cotangent=cotangent, seg_ids=seg_ids, mix_weight=mix_weight, out_weight=out_weight, gate_weight=gate_weight, up_weight=up_weight, down_weight=down_weight, first_gain=first_gain, first_shift=first_shift, second_gain=second_gain, second_shift=second_shift)


@jax.custom_vjp
def low(v):
    return lax.optimization_barrier(v.astype(jnp.bfloat16)).astype(jnp.float32)

@jax.custom_vjp
def low_back(v):
    return v

def low_keep(v):
    return (low(v), None)

def low_pass(kept, grad):
    return (grad,)

def back_keep(v):
    return (v, None)

def back_low(kept, grad):
    return (low(grad),)
low.defvjp(low_keep, low_pass)
low_back.defvjp(back_keep, back_low)
highest = lax.Precision.HIGHEST
norm_epsilon = 1e-05
masked_score = -1e+30
rotary_base = 1000.0

def doc_positions(seg_rows):
    length = seg_rows.shape[-1]
    places = jnp.broadcast_to(jnp.arange(length, dtype=jnp.int32), seg_rows.shape)
    change = jnp.concatenate([jnp.ones(seg_rows.shape[:-1] + (1,), jnp.int32), (seg_rows[..., 1:] != seg_rows[..., :-1]).astype(jnp.int32)], axis=-1)
    starts = lax.cummax(jnp.where(change > 0, places, 0), axis=seg_rows.ndim - 1)
    return (places - starts).astype(jnp.int32)

def rotary_tables(positions, head_dim):
    half_dim = head_dim // 2
    freqs = rotary_base ** (-2.0 * jnp.arange(half_dim, dtype=jnp.float32) / head_dim)
    angles = positions.astype(jnp.float32)[..., None] * freqs
    cosine = jnp.cos(angles)
    sine = jnp.sin(angles)
    return (jnp.concatenate([cosine, cosine], axis=-1), jnp.concatenate([sine, sine], axis=-1))

def rotate(vectors, cosine, sine):
    half_dim = vectors.shape[-1] // 2
    turned = jnp.concatenate([-vectors[..., half_dim:], vectors[..., :half_dim]], axis=-1)
    return vectors * cosine[..., None, :] + turned * sine[..., None, :]

def layer_norm(values, gain, shift):
    centered = values - lax.optimization_barrier(jnp.mean(values, axis=-1, keepdims=True))
    scale_inv = lax.rsqrt(lax.optimization_barrier(jnp.mean(centered * centered, axis=-1, keepdims=True)) + norm_epsilon)
    return centered * scale_inv * gain + shift

def layer_forward(token_row, mix_weight, out_weight, gate_weight, up_weight, down_weight, first_gain, first_shift, second_gain, second_shift, seg_row):
    length = token_row.shape[0]
    width = token_row.shape[1]
    head_count = width // HEAD_DIM
    cosine, sine = rotary_tables(doc_positions(seg_row), HEAD_DIM)
    mixed = low_back(jnp.dot(token_row, mix_weight, precision=highest)).reshape(length, 3, head_count, HEAD_DIM)
    queries = low(rotate(mixed[:, 0], cosine, sine))
    key_vectors = low(rotate(mixed[:, 1], cosine, sine))
    values = low(mixed[:, 2])
    scores = low_back(jnp.einsum('qhd,khd->hqk', queries, key_vectors, precision=highest) * HEAD_DIM ** (-0.5))
    same_doc = seg_row[:, None] == seg_row[None, :]
    scores = jnp.where(same_doc[None], scores, masked_score)
    row_max = lax.optimization_barrier(jnp.max(scores, axis=-1, keepdims=True))
    exponent = jnp.exp(scores - row_max)
    probs = low(exponent / lax.optimization_barrier(jnp.sum(exponent, axis=-1, keepdims=True)))
    attended = jnp.einsum('hqk,khd->qhd', probs, values, precision=highest).reshape(length, width)
    attended = low(low_back(attended))
    branch = low_back(jnp.dot(attended, out_weight, precision=highest))
    normed_one = layer_norm(token_row + branch, first_gain, first_shift)
    ffn_in = low(normed_one)
    gate = low_back(jnp.dot(ffn_in, gate_weight, precision=highest))
    upper = low_back(jnp.dot(ffn_in, up_weight, precision=highest))
    hidden = low(gate / (1.0 + jnp.exp(-gate)) * upper)
    ffn_out = low_back(jnp.dot(hidden, down_weight, precision=highest))
    return layer_norm(normed_one + ffn_out, second_gain, second_shift)

def reference(tokens, cotangent, seg_ids, mix_weight, out_weight, gate_weight, up_weight, down_weight, first_gain, first_shift, second_gain, second_shift):
    weights = tuple((weight.astype(jnp.float32) for weight in (mix_weight, out_weight, gate_weight, up_weight, down_weight, first_gain, first_shift, second_gain, second_shift)))

    def per_row(totals, pieces):
        token_row, grad_row, seg_row = pieces

        def forward(row_in, *params):
            return layer_forward(row_in, *params, seg_row)
        result, pullback = jax.vjp(forward, token_row.astype(jnp.float32), *weights)
        grads = pullback(grad_row.astype(jnp.float32))
        updated = tuple((total_part + grad_part for total_part, grad_part in zip(totals, grads[1:])))
        return (updated, (result, grads[0]))
    start = tuple((jnp.zeros(weight.shape, jnp.float32) for weight in weights))
    totals, (outputs, input_grads) = lax.scan(per_row, start, (tokens, cotangent, seg_ids))
    return (outputs, input_grads, totals[0], totals[1], totals[2], totals[3], totals[4], totals[5], totals[6], totals[7], totals[8])
```

```python
import functools

import jax
import jax.numpy as jnp
from jax import lax
from jax.experimental import pallas as pl
from jax.experimental.pallas import tpu as pltpu
from jax.sharding import PartitionSpec as P

HEAD_DIM = 64


norm_epsilon = 1e-05
masked_score = -1e30
rotary_base = 1000.0


def shortened(x):
    return jax.tree.map(lambda a: a.astype(jnp.bfloat16) if a.dtype == jnp.float32 else a, x)


def doc_positions(seg_rows):
    length = seg_rows.shape[-1]
    places = jnp.broadcast_to(jnp.arange(length, dtype=jnp.int32), seg_rows.shape)
    change = jnp.concatenate(
        [
            jnp.ones(seg_rows.shape[:-1] + (1,), jnp.int32),
            (seg_rows[..., 1:] != seg_rows[..., :-1]).astype(jnp.int32),
        ],
        axis=-1,
    )
    starts = lax.cummax(jnp.where(change > 0, places, 0), axis=seg_rows.ndim - 1)
    return places - starts


def rotary_tables(positions, head_dim):
    half_dim = head_dim // 2
    freqs = rotary_base ** (-2.0 * jnp.arange(half_dim, dtype=jnp.float32) / head_dim)
    angles = positions.astype(jnp.float32)[..., None] * freqs
    cosine = jnp.cos(angles)
    sine = jnp.sin(angles)
    return (jnp.concatenate([cosine, cosine], axis=-1), jnp.concatenate([sine, sine], axis=-1))


def rotate(vectors, cosine, sine):
    half_dim = vectors.shape[-1] // 2
    turned = jnp.concatenate([-vectors[..., half_dim:], vectors[..., :half_dim]], axis=-1)
    return vectors * cosine[..., None, :] + turned * sine[..., None, :]


def rotate_back(grads, cosine, sine):
    half_dim = grads.shape[-1] // 2
    scaled = grads * sine[..., None, :]
    turned = jnp.concatenate([scaled[..., half_dim:], -scaled[..., :half_dim]], axis=-1)
    return grads * cosine[..., None, :] + turned


def layer_norm(values, gain, shift):
    centered = values - jnp.mean(values, axis=-1, keepdims=True)
    scale_inv = lax.rsqrt(jnp.mean(centered * centered, axis=-1, keepdims=True) + norm_epsilon)
    normed = centered * scale_inv
    return (normed * gain + shift, normed, scale_inv)


def norm_back(grad, normed, scale_inv, gain):
    scaled = grad * gain
    return scale_inv * (
        scaled
        - jnp.mean(scaled, axis=-1, keepdims=True)
        - normed * jnp.mean(scaled * normed, axis=-1, keepdims=True)
    )


def dot_last(left, right):
    return lax.dot_general(
        left, right, (((1,), (1,)), ((), ())), preferred_element_type=jnp.float32
    )


def dot_first(left, right):
    return lax.dot_general(
        left, right, (((0,), (0,)), ((), ())), preferred_element_type=jnp.float32
    )


def masked_scores(query_part, key_vectors, seg_part, seg_row, score_scale):
    scores = (
        jnp.einsum("qhd,khd->hqk", query_part, key_vectors, preferred_element_type=jnp.float32)
        * score_scale
    )
    return jnp.where((seg_part[:, None] == seg_row[None, :])[None], scores, masked_score)


def attend_row(queries, key_vectors, values, seg_row):
    length, head_count, head_dim = queries.shape
    block_rows = min(512, length)
    block_count = length // block_rows
    score_scale = head_dim ** (-0.5)

    def one_block(pieces):
        query_part, seg_part = pieces
        scores = masked_scores(query_part, key_vectors, seg_part, seg_row, score_scale)
        row_max = jnp.max(scores, axis=-1, keepdims=True)
        exponent = jnp.exp(scores - row_max)
        row_sum = jnp.sum(exponent, axis=-1, keepdims=True)
        prob_low = (exponent / row_sum).astype(jnp.bfloat16)
        attended = jnp.einsum("hqk,khd->qhd", prob_low, values, preferred_element_type=jnp.float32)
        return (attended, (row_max + jnp.log(row_sum))[..., 0])

    attended, log_total = lax.map(
        one_block,
        (
            queries.reshape(block_count, block_rows, head_count, head_dim),
            seg_row.reshape(block_count, block_rows),
        ),
    )
    return (attended.reshape(length, head_count, head_dim), log_total)


def attend_back(queries, key_vectors, values, seg_row, d_attended, log_total):
    length, head_count, head_dim = queries.shape
    block_rows = min(512, length)
    block_count = length // block_rows
    score_scale = head_dim ** (-0.5)

    def one_block(carry, pieces):
        key_acc, value_acc = carry
        query_part, grad_part, total_part, seg_part = pieces
        scores = masked_scores(query_part, key_vectors, seg_part, seg_row, score_scale)
        probs = jnp.exp(scores - total_part[..., None])
        value_acc = value_acc + jnp.einsum(
            "hqk,qhd->khd",
            probs.astype(jnp.bfloat16),
            grad_part,
            preferred_element_type=jnp.float32,
        )
        d_probs = jnp.einsum("qhd,khd->hqk", grad_part, values, preferred_element_type=jnp.float32)
        centre = jnp.sum(probs * d_probs, axis=-1, keepdims=True)
        d_scores = (probs * (d_probs - centre)).astype(jnp.bfloat16)
        query_grad = (
            jnp.einsum("hqk,khd->qhd", d_scores, key_vectors, preferred_element_type=jnp.float32)
            * score_scale
        )
        key_acc = (
            key_acc
            + jnp.einsum("hqk,qhd->khd", d_scores, query_part, preferred_element_type=jnp.float32)
            * score_scale
        )
        return ((key_acc, value_acc), query_grad)

    zeros = jnp.zeros((length, head_count, head_dim), jnp.float32)
    pieces = (
        queries.reshape(block_count, block_rows, head_count, head_dim),
        d_attended.reshape(block_count, block_rows, head_count, head_dim),
        log_total,
        seg_row.reshape(block_count, block_rows),
    )
    (key_grad, value_grad), query_grad = lax.scan(one_block, (zeros, zeros), pieces)
    return (query_grad.reshape(length, head_count, head_dim), key_grad, value_grad)


def shards(
    tokens,
    cotangent,
    seg_ids,
    mix_weight,
    out_weight,
    gate_weight,
    up_weight,
    down_weight,
    first_gain,
    first_shift,
    second_gain,
    second_shift,
):
    tensor_count = lax.axis_size("tensor")
    tensor_index = lax.axis_index("tensor")
    data_count = lax.axis_size("dp")
    row_count, shard_len, width = tokens.shape
    seq_len = shard_len * tensor_count
    head_dim = HEAD_DIM
    head_count = width // head_dim
    flat_rows = row_count * seq_len
    own_start = tensor_index * shard_len
    whole = lax.all_gather(tokens, "tensor", axis=1, tiled=True)
    mix_full, out_full, gain_one, shift_one, gain_two, shift_two = (
        lax.all_gather(mix_weight, ("dp", "tensor"), axis=0, tiled=True),
        lax.all_gather(out_weight, ("dp", "tensor"), axis=0, tiled=True),
        lax.all_gather(first_gain, ("dp", "tensor"), axis=0, tiled=True),
        lax.all_gather(first_shift, ("dp", "tensor"), axis=0, tiled=True),
        lax.all_gather(second_gain, ("dp", "tensor"), axis=0, tiled=True),
        lax.all_gather(second_shift, ("dp", "tensor"), axis=0, tiled=True),
    )
    gate_full, up_full, down_full = (
        lax.all_gather(gate_weight, "dp", axis=0, tiled=True),
        lax.all_gather(up_weight, "dp", axis=0, tiled=True),
        lax.all_gather(down_weight, "dp", axis=1, tiled=True),
    )
    gain_one = gain_one.astype(jnp.float32)
    shift_one = shift_one.astype(jnp.float32)
    gain_two = gain_two.astype(jnp.float32)
    shift_two = shift_two.astype(jnp.float32)
    flat_in = whole.reshape(flat_rows, width)
    mixed = jnp.dot(flat_in, mix_full, preferred_element_type=jnp.float32).reshape(
        row_count, seq_len, 3, head_count, head_dim
    )
    cosine, sine = rotary_tables(doc_positions(seg_ids), head_dim)
    queries = rotate(mixed[:, :, 0], cosine, sine).astype(jnp.bfloat16)
    key_vectors = rotate(mixed[:, :, 1], cosine, sine).astype(jnp.bfloat16)
    values = mixed[:, :, 2].astype(jnp.bfloat16)
    attended, log_total = lax.map(
        lambda pieces: attend_row(*pieces), (queries, key_vectors, values, seg_ids)
    )
    attended_low = attended.reshape(flat_rows, width).astype(jnp.bfloat16)
    branch = jnp.dot(attended_low, out_full, preferred_element_type=jnp.float32)
    first = flat_in.astype(jnp.float32) + branch
    normed_one, unit_one, inv_one = layer_norm(first, gain_one, shift_one)
    ffn_in = normed_one.astype(jnp.bfloat16)
    gate = jnp.dot(ffn_in, gate_full, preferred_element_type=jnp.float32)
    upper = jnp.dot(ffn_in, up_full, preferred_element_type=jnp.float32)
    sigma = 1.0 / (1.0 + jnp.exp(-gate))
    swish = gate * sigma
    hidden = (swish * upper).astype(jnp.bfloat16)
    partial_out = jnp.dot(hidden, down_full, preferred_element_type=jnp.float32).reshape(
        row_count, seq_len, width
    )
    ffn_out = lax.psum_scatter(
        partial_out.astype(jnp.bfloat16), "tensor", scatter_dimension=1, tiled=True
    ).astype(jnp.float32)
    own_normed = lax.dynamic_slice_in_dim(
        normed_one.reshape(row_count, seq_len, width), own_start, shard_len, 1
    )
    output, unit_two, inv_two = layer_norm(own_normed + ffn_out, gain_two, shift_two)
    grad_output = cotangent.astype(jnp.float32)
    d_second = norm_back(grad_output, unit_two, inv_two, gain_two)
    second_gain_part = jnp.sum(grad_output * unit_two, axis=(0, 1))
    second_shift_part = jnp.sum(grad_output, axis=(0, 1))
    d_ffn_full = lax.all_gather(
        d_second.astype(jnp.bfloat16), "tensor", axis=1, tiled=True
    ).reshape(flat_rows, width)
    gate_back, up_back, down_back = (
        lax.all_gather(gate_weight, "dp", axis=0, tiled=True),
        lax.all_gather(up_weight, "dp", axis=0, tiled=True),
        lax.all_gather(down_weight, "dp", axis=1, tiled=True),
    )
    d_hidden = dot_last(d_ffn_full, down_back)
    d_up_low = (d_hidden * swish).astype(jnp.bfloat16)
    d_gate_low = (d_hidden * upper * sigma * (1.0 + gate * (1.0 - sigma))).astype(jnp.bfloat16)
    grad_down_part = dot_first(hidden, d_ffn_full)
    grad_gate_part = dot_first(ffn_in, d_gate_low)
    grad_up_part = dot_first(ffn_in, d_up_low)
    d_normed_part = (dot_last(d_gate_low, gate_back) + dot_last(d_up_low, up_back)).reshape(
        row_count, seq_len, width
    )
    own_rows = lax.dynamic_slice_in_dim(d_normed_part, own_start, shard_len, 1) + d_second
    d_normed_part = lax.dynamic_update_slice_in_dim(d_normed_part, own_rows, own_start, 1)
    d_normed, second_gain_grad, second_shift_grad = lax.psum(
        (d_normed_part, second_gain_part, second_shift_part), "tensor"
    )
    d_normed = d_normed.reshape(flat_rows, width)
    d_first = norm_back(d_normed, unit_one, inv_one, gain_one)
    first_gain_grad = jnp.sum(d_normed * unit_one, axis=0)
    first_shift_grad = jnp.sum(d_normed, axis=0)
    d_branch_low = d_first.astype(jnp.bfloat16)
    own_first = lax.dynamic_slice_in_dim(
        d_first.reshape(row_count, seq_len, width), own_start, shard_len, 1
    )
    norm_parts = (first_gain_grad, first_shift_grad, second_gain_grad, second_shift_grad)
    grad_gate, grad_up, grad_down = (
        lax.psum_scatter(
            grad_gate_part.astype(jnp.bfloat16), "dp", scatter_dimension=0, tiled=True
        ).astype(jnp.float32),
        lax.psum_scatter(
            grad_up_part.astype(jnp.bfloat16), "dp", scatter_dimension=0, tiled=True
        ).astype(jnp.float32),
        lax.psum_scatter(
            grad_down_part.astype(jnp.bfloat16), "dp", scatter_dimension=1, tiled=True
        ).astype(jnp.float32),
    )
    mix_back, out_back = (
        lax.all_gather(mix_weight, ("dp", "tensor"), axis=0, tiled=True),
        lax.all_gather(out_weight, ("dp", "tensor"), axis=0, tiled=True),
    )
    grad_out_part = dot_first(attended_low, d_branch_low)
    d_attended = (
        dot_last(d_branch_low, out_back)
        .astype(jnp.bfloat16)
        .reshape(row_count, seq_len, head_count, head_dim)
    )
    query_grad, key_grad, value_grad = lax.map(
        lambda pieces: attend_back(*pieces),
        (queries, key_vectors, values, seg_ids, d_attended, log_total),
    )
    d_mixed = (
        jnp.stack(
            [
                rotate_back(query_grad, cosine, sine),
                rotate_back(key_grad, cosine, sine),
                value_grad,
            ],
            axis=2,
        )
        .astype(jnp.bfloat16)
        .reshape(flat_rows, 3 * width)
    )
    grad_mix_part = dot_first(flat_in, d_mixed)
    own_mixed = lax.dynamic_slice_in_dim(
        d_mixed.reshape(row_count, seq_len, 3 * width), own_start, shard_len, 1
    ).reshape(row_count * shard_len, 3 * width)
    grad_tokens = own_first + dot_last(own_mixed, mix_back).reshape(row_count, shard_len, width)
    matrix_parts = (grad_mix_part, grad_out_part)
    attn_parts = matrix_parts + tuple(norm_parts)
    owned = width // (data_count * tensor_count)
    summed = jax.tree.map(
        lambda part: part.astype(jnp.float32),
        lax.psum_scatter(shortened(attn_parts), "dp", scatter_dimension=0, tiled=True),
    )
    results = tuple(
        (lax.dynamic_slice_in_dim(part, tensor_index * owned, owned, 0) for part in summed)
    )
    norm_results = results[2:]
    return (
        output,
        grad_tokens,
        results[0],
        results[1],
        grad_gate,
        grad_up,
        grad_down,
        norm_results[0],
        norm_results[1],
        norm_results[2],
        norm_results[3],
    )


def nn(a, b):
    return lax.dot_general(a, b, (((1,), (0,)), ((), ())), preferred_element_type=jnp.float32)


def nt(a, b):
    return lax.dot_general(a, b, (((1,), (1,)), ((), ())), preferred_element_type=jnp.float32)


def tn(a, b):
    return lax.dot_general(a, b, (((0,), (0,)), ((), ())), preferred_element_type=jnp.float32)


VM = pl.BlockSpec(memory_space=pltpu.VMEM)
SM = pl.BlockSpec(memory_space=pltpu.SMEM)
HB = pl.BlockSpec(memory_space=pl.ANY)
BLK = 256
WORST = -1e30


def sds(shape, dtype=jnp.bfloat16):
    return jax.ShapeDtypeStruct(shape, dtype)


def cost(flops, moved, exps=0):
    return pl.CostEstimate(flops=int(flops), bytes_accessed=int(moved), transcendentals=int(exps))


def swap_halves(z):
    lane = lax.broadcasted_iota(jnp.int32, z.shape, 1)
    return jnp.where((lane & 32) == 0, pltpu.roll(z, 96, 1), pltpu.roll(z, 32, 1))


def gather_rows(pieces, dest, own, sems):
    rows = pieces[0].shape[0]
    copies = [
        pltpu.make_async_copy(piece, dest.at[pl.ds(pl.multiple_of((own ^ k) * rows, rows), rows), :], sems.at[k])
        for k, piece in enumerate(pieces)
    ]
    for copy in copies:
        copy.start()
    for copy in copies:
        copy.wait()


def attend_kernel(heads, shard, scal, *refs):
    mix_parts, toks = refs[:8], refs[8:12]
    cos_ref, sin_ref, segc_ref, segr_ref = refs[12:16]
    q_ref, k_ref, v_ref = refs[16:19]
    o_refs = refs[19:23]
    lse_ref, mix_ref, o_scr, acc_ref, sems = refs[23:]
    t, d = scal[0], scal[1]
    gather_rows(mix_parts, mix_ref, d, sems)
    for p in range(4):
        for half in range(shard // BLK):
            y = nn(toks[p][half * BLK : (half + 1) * BLK, :], mix_ref[...])
            row = pl.multiple_of((t ^ p) * shard + half * BLK, BLK)
            c, s = cos_ref[pl.ds(row, BLK), :], sin_ref[pl.ds(row, BLK), :]
            parts = []
            for g in range(3):
                z = y[:, 128 * g : 128 * (g + 1)]
                z = z * c + swap_halves(z) * s
                parts += [z[:, :64], z[:, 64:]]
            rows = pl.ds(p * shard + half * BLK, BLK)
            for h in range(heads):
                q_ref[h, rows, :] = (parts[h].astype(jnp.bfloat16) * 0.125).astype(jnp.bfloat16)
                k_ref[h, rows, :] = parts[heads + h].astype(jnp.bfloat16)
                v_ref[h, rows, :] = y[:, 384 + 64 * h : 448 + 64 * h].astype(jnp.bfloat16)

    per = shard // BLK

    def place(b):
        return (b // per) ^ t, b % per

    def q_block(i, _):
        p, half = place(i)
        q_row = pl.multiple_of(p * shard + half * BLK, BLK)
        seg_q = segr_ref[pl.ds(i, 1), :]
        acc_ref[...] = jnp.zeros_like(acc_ref)

        def k_block(j, carry):
            kp, khalf = place(j)
            k_row = pl.multiple_of(kp * shard + khalf * BLK, BLK)
            seg_k = segc_ref[pl.ds(pl.multiple_of(j * BLK, BLK), BLK), :]
            bias = jnp.where(seg_k == seg_q, 0.0, WORST)
            new = []
            for h in range(heads):
                m, l = carry[2 * h], carry[2 * h + 1]
                s = nt(k_ref[h, pl.ds(k_row, BLK), :], q_ref[h, pl.ds(q_row, BLK), :]) + bias
                m_new = jnp.maximum(m, jnp.max(s, axis=0, keepdims=True))
                e = jnp.exp(s - m_new)
                a = jnp.exp(m - m_new)
                l = a * l + jnp.sum(e, axis=0, keepdims=True)
                acc_ref[h] = acc_ref[h] * a + tn(v_ref[h, pl.ds(k_row, BLK), :], e.astype(jnp.bfloat16))
                new += [m_new, l]
            return tuple(new)

        start = (jnp.full((1, BLK), WORST, jnp.float32), jnp.zeros((1, BLK), jnp.float32)) * heads
        stats = lax.fori_loop(scal[2 + i], scal[10 + i], k_block, start)
        lanes = pl.ds(pl.multiple_of(half * BLK, BLK), BLK)
        for h in range(heads):
            m, l = stats[2 * h], stats[2 * h + 1]
            o_scr[p, 64 * h : 64 * (h + 1), lanes] = (acc_ref[h] / l).astype(jnp.bfloat16)
            lse_ref[p, h : h + 1, lanes] = m + jnp.log(l)
        return 0

    lax.fori_loop(0, 4 * per, q_block, 0)
    for p in range(4):
        o_refs[p][...] = o_scr[p]


def attend(scal, mix_parts, toks, cosine, sine, seg_col, seg_row, heads):
    shard, width = toks[0].shape
    seq, cols = 4 * shard, 3 * heads * 64
    outs = [sds((heads, seq, 64))] * 3 + [sds((heads * 64, shard))] * 4
    outs += [sds((4, 8, shard), jnp.float32), sds((width, cols))]
    return pl.pallas_call(
        functools.partial(attend_kernel, heads, shard),
        out_shape=outs,
        in_specs=[SM] + [HB] * 8 + [VM] * 8,
        out_specs=[VM] * len(outs),
        scratch_shapes=[
            pltpu.VMEM((4, heads * 64, shard), jnp.bfloat16),
            pltpu.VMEM((heads, 64, BLK), jnp.float32),
            pltpu.SemaphoreType.DMA((8,)),
        ],
        cost_estimate=cost(2 * seq * width * cols + 4 * 2 * seq * seq * 64 * heads, 20e6, seq * seq * heads / 2),
        name="attend",
    )(scal, *mix_parts, *toks, cosine, sine, seg_col, seg_row)


def branch_kernel(scal, r0, r1, r2, r3, tok_ref, *refs):
    out_parts = refs[:8]
    ffn_ref, unit_ref, inv_ref, out_ref, par_ref, sems = refs[8:]
    t, d = scal[0], scal[1]
    width = tok_ref.shape[1]
    gather_rows(out_parts, out_ref, d, sems)
    par = jnp.transpose(out_ref[:, width:].astype(jnp.float32))[:8]
    par_ref[...] = par
    gain, shift = par[0:1], par[1:2]
    rows_of = r0.shape[0]
    for half in range(tok_ref.shape[0] // BLK):
        rows = slice(half * BLK, (half + 1) * BLK)
        first = tok_ref[rows, :].astype(jnp.float32)
        for k, r in enumerate((r0, r1, r2, r3)):
            at = pl.multiple_of((t ^ k) * rows_of, rows_of)
            first = first + tn(r[:, rows], out_ref[pl.ds(at, rows_of), :width])
        centred = first - jnp.mean(first, axis=-1, keepdims=True)
        inv = lax.rsqrt(jnp.mean(centred * centred, axis=-1, keepdims=True) + norm_epsilon)
        unit = centred * inv
        unit_ref[rows, :] = unit
        inv_ref[rows, :] = inv
        ffn_ref[rows, :] = (unit * gain + shift).astype(jnp.bfloat16)


def branch(scal, att, tokens, out_parts):
    shard, width = tokens.shape
    wide = out_parts[0].shape[1]
    return pl.pallas_call(
        branch_kernel,
        out_shape=[
            sds((shard, width)),
            sds((shard, width), jnp.float32),
            sds((shard, 1), jnp.float32),
            sds((width, wide)),
            sds((8, width), jnp.float32),
        ],
        in_specs=[SM] + [VM] * 5 + [HB] * 8,
        out_specs=[VM] * 5,
        scratch_shapes=[pltpu.SemaphoreType.DMA((8,))],
        cost_estimate=cost(2 * shard * width * width, 7e6),
        name="branch",
    )(scal, *att, tokens, *out_parts)


def join_kernel(count, scal, *refs):
    parts, (out_ref, sems) = refs[:8], refs[8:]
    d = scal[1]
    rows = parts[0].shape[1]
    copies = []
    for k in range(8):
        at = pl.ds(pl.multiple_of((d ^ k) * rows, rows), rows)
        copies.append(pltpu.make_async_copy(parts[k], out_ref.at[:, at, :], sems.at[k]))
    for copy in copies:
        copy.start()
    for copy in copies:
        copy.wait()


def join(scal, parts):
    count, rows, cols = parts[0].shape
    return pl.pallas_call(
        functools.partial(join_kernel, count),
        out_shape=sds((count, 8 * rows, cols)),
        in_specs=[SM] + [HB] * 8,
        out_specs=VM,
        scratch_shapes=[pltpu.SemaphoreType.DMA((8,))],
        cost_estimate=cost(0, 4 * count * 8 * rows * cols),
        name="join",
    )(scal, *parts)


def ffn_kernel(per, xa, xb, w_ref, gate_ref, up_ref, hid_ref, pa, pb):
    i = pl.program_id(0)
    x = jnp.where(i < per, xa[...], xb[...])
    gate = nn(x, w_ref[0])
    upper = nn(x, w_ref[1])
    hidden = (gate / (1.0 + jnp.exp(-gate)) * upper).astype(jnp.bfloat16)
    gate_ref[...] = gate.astype(jnp.bfloat16)
    up_ref[...] = upper.astype(jnp.bfloat16)
    hid_ref[...] = hidden
    part = nt(hidden, w_ref[2]).astype(jnp.bfloat16)

    @pl.when(i < per)
    def _():
        pa[...] = part

    @pl.when(i >= per)
    def _():
        pb[...] = part


def pair_specs(per, width):
    first = pl.BlockSpec((BLK, width), lambda i: (jnp.minimum(i, per - 1), 0))
    second = pl.BlockSpec((BLK, width), lambda i: (jnp.maximum(i - per, 0), 0))
    both = pl.BlockSpec((BLK, width), lambda i: (i, 0))
    return first, second, both


def ffn(xa, xb, weights):
    shard, width = xa.shape
    hid = weights.shape[2]
    per = shard // BLK
    first, second, both = pair_specs(per, width)
    _, _, both_h = pair_specs(per, hid)
    return pl.pallas_call(
        functools.partial(ffn_kernel, per),
        grid=(2 * per,),
        out_shape=[sds((2 * shard, hid))] * 3 + [sds((shard, width))] * 2,
        in_specs=[first, second, pl.BlockSpec(weights.shape, lambda i: (0, 0, 0), pipeline_mode=pl.Buffered(1))],
        out_specs=[both_h] * 3 + [first, second],
        cost_estimate=cost(12 * shard * width * hid, 12e6),
        name="ffn",
    )(xa, xb, weights)


def second_kernel(own, r1, r2, unit1, par_ref, cot_ref, out_ref, dsec_ref, dlow_ref, norm_ref):
    par = par_ref[...]
    added = own[...].astype(jnp.float32) + r1[...].astype(jnp.float32) + r2[...].astype(jnp.float32)
    total = unit1[...] * par[0:1] + par[1:2] + added
    centred = total - jnp.mean(total, axis=-1, keepdims=True)
    inv = lax.rsqrt(jnp.mean(centred * centred, axis=-1, keepdims=True) + norm_epsilon)
    unit = centred * inv
    out_ref[...] = unit * par[2:3] + par[3:4]
    y = cot_ref[...].astype(jnp.float32)
    dn = y * par[2:3]
    dsec = inv * (dn - jnp.mean(dn, axis=-1, keepdims=True) - unit * jnp.mean(dn * unit, axis=-1, keepdims=True))
    dsec_ref[...] = dsec
    dlow_ref[...] = dsec.astype(jnp.bfloat16)

    @pl.when(pl.program_id(0) == 0)
    def _():
        norm_ref[...] = jnp.zeros_like(norm_ref)

    norm_ref[0:1, :] += jnp.sum(y * unit, axis=0, keepdims=True)
    norm_ref[1:2, :] += jnp.sum(y, axis=0, keepdims=True)


def second(own, r1, r2, unit1, par, cot):
    shard, width = own.shape
    rows = 128
    tile = pl.BlockSpec((rows, width), lambda i: (i, 0))
    whole = pl.BlockSpec((8, width), lambda i: (0, 0))
    return pl.pallas_call(
        second_kernel,
        grid=(shard // rows,),
        out_shape=[
            sds((shard, width), jnp.float32),
            sds((shard, width), jnp.float32),
            sds((shard, width)),
            sds((8, width), jnp.float32),
        ],
        in_specs=[tile] * 4 + [whole, tile],
        out_specs=[tile] * 3 + [whole],
        cost_estimate=cost(30 * shard * width, 9e6),
        name="second",
    )(own, r1, r2, unit1, par, cot)


def ffn_back_kernel(per, da, db, gate_ref, up_ref, w_ref, dg_ref, du_ref, pa, pb):
    i = pl.program_id(0)
    dlow = jnp.where(i < per, da[...], db[...])
    d_hidden = nn(dlow, w_ref[2])
    gate, upper = gate_ref[...].astype(jnp.float32), up_ref[...].astype(jnp.float32)
    sigma = 1.0 / (1.0 + jnp.exp(-gate))
    du = (d_hidden * gate * sigma).astype(jnp.bfloat16)
    dg = (d_hidden * upper * sigma * (1.0 + gate * (1.0 - sigma))).astype(jnp.bfloat16)
    du_ref[...] = du
    dg_ref[...] = dg
    part = (nt(dg, w_ref[0]) + nt(du, w_ref[1])).astype(jnp.bfloat16)

    @pl.when(i < per)
    def _():
        pa[...] = part

    @pl.when(i >= per)
    def _():
        pb[...] = part


def ffn_back(da, db, gate, upper, weights):
    shard, width = da.shape
    hid = weights.shape[2]
    per = shard // BLK
    first, second_, _ = pair_specs(per, width)
    _, _, both_h = pair_specs(per, hid)
    return pl.pallas_call(
        functools.partial(ffn_back_kernel, per),
        grid=(2 * per,),
        out_shape=[sds((2 * shard, hid))] * 2 + [sds((shard, width))] * 2,
        in_specs=[first, second_, both_h, both_h, pl.BlockSpec(weights.shape, lambda i: (0, 0, 0), pipeline_mode=pl.Buffered(1))],
        out_specs=[both_h] * 2 + [first, second_],
        cost_estimate=cost(12 * shard * width * hid, 12e6),
        name="ffn_back",
    )(da, db, gate, upper, weights)


def ffn_grad_kernel(scal, *refs):
    xs, ds = refs[:4], refs[4:8]
    hids, dgs, dus = refs[8:10], refs[10:12], refs[12:14]
    even, odd, xt, dt, scr = refs[14:]
    d = scal[1]
    shard = xs[0].shape[0]

    @pl.when(pl.program_id(0) == 0)
    def _():
        for p in range(4):
            xt[:, p * shard : (p + 1) * shard] = jnp.transpose(xs[p][...])
            dt[:, p * shard : (p + 1) * shard] = jnp.transpose(ds[p][...])

    half = 2 * shard
    for w, (left, right) in enumerate(((xt, dgs), (xt, dus), (dt, hids))):
        grad = nn(left[:, :half], right[0][...]) + nn(left[:, half:], right[1][...])
        for block in range(8):
            rows = grad.shape[0] // 8
            k = d ^ block
            scr[(k & 1) * 4 + (k >> 1), w] = grad[block * rows : (block + 1) * rows].astype(jnp.bfloat16)
    even[...] = scr[0:4]
    odd[...] = scr[4:8]


def ffn_grad(scal, xs, ds, hids, dgs, dus):
    shard, width = xs[0].shape
    hid = hids[0].shape[1]
    tile = 256
    rows = width // 8
    col = pl.BlockSpec((2 * shard, tile), lambda i: (0, i))
    out = pl.BlockSpec((4, 3, rows, tile), lambda i: (0, 0, 0, i))
    return pl.pallas_call(
        ffn_grad_kernel,
        grid=(hid // tile,),
        out_shape=[sds((4, 3, rows, hid))] * 2,
        in_specs=[SM] + [VM] * 8 + [col] * 6,
        out_specs=[out] * 2,
        scratch_shapes=[
            pltpu.VMEM((width, 4 * shard), jnp.bfloat16),
            pltpu.VMEM((width, 4 * shard), jnp.bfloat16),
            pltpu.VMEM((8, 3, rows, tile), jnp.bfloat16),
        ],
        cost_estimate=cost(6 * 4 * shard * width * hid, 20e6),
        name="ffn_grad",
    )(scal, *xs, *ds, *hids, *dgs, *dus)


def first_kernel(scal, own, r1, r2, dsec_ref, unit_ref, inv_ref, par_ref, out_ref, dfirst_ref, dbr_ref, a0, a1, a2, a3, norm_ref):
    t = scal[0]
    y = own[...].astype(jnp.float32) + r1[...].astype(jnp.float32) + r2[...].astype(jnp.float32) + dsec_ref[...]
    unit = unit_ref[...]
    dn = y * par_ref[0:1, :]
    dfirst = inv_ref[...] * (
        dn - jnp.mean(dn, axis=-1, keepdims=True) - unit * jnp.mean(dn * unit, axis=-1, keepdims=True)
    )
    dfirst_ref[...] = dfirst
    dbr = dfirst.astype(jnp.bfloat16)
    dbr_ref[...] = dbr
    rows_of, width = a0.shape[0], own.shape[1]
    for k, a in enumerate((a0, a1, a2, a3)):
        at = pl.multiple_of((t ^ k) * rows_of, rows_of)
        a[...] = nt(out_ref[pl.ds(at, rows_of), :width], dbr).astype(jnp.bfloat16)

    @pl.when(pl.program_id(0) == 0)
    def _():
        norm_ref[...] = jnp.zeros_like(norm_ref)

    norm_ref[0:1, :] += jnp.sum(y * unit, axis=0, keepdims=True)
    norm_ref[1:2, :] += jnp.sum(y, axis=0, keepdims=True)


def first_back(scal, own, r1, r2, dsec, unit, inv, par, out_full):
    shard, width = own.shape
    rows_of = width // 4
    tile = pl.BlockSpec((BLK, width), lambda i: (i, 0))
    whole = pl.BlockSpec((8, width), lambda i: (0, 0))
    lane = pl.BlockSpec((rows_of, BLK), lambda i: (0, i))
    return pl.pallas_call(
        first_kernel,
        grid=(shard // BLK,),
        out_shape=[sds((shard, width), jnp.float32), sds((shard, width))]
        + [sds((rows_of, shard))] * 4
        + [sds((8, width), jnp.float32)],
        in_specs=[SM] + [tile] * 5
        + [
            pl.BlockSpec((BLK, 1), lambda i: (i, 0)),
            whole,
            pl.BlockSpec(out_full.shape, lambda i: (0, 0), pipeline_mode=pl.Buffered(1)),
        ],
        out_specs=[tile] * 2 + [lane] * 4 + [whole],
        cost_estimate=cost(2 * shard * width * width, 10e6),
        name="first_back",
    )(scal, own, r1, r2, dsec, unit, inv, par, out_full)


def out_grad_kernel(scal, r0, r1, r2, r3, dbr_ref, n1_ref, n2_ref, even, odd, full, scr):
    t, d = scal[0], scal[1]
    rows_of, width = r0.shape[0], dbr_ref.shape[1]
    for k, r in enumerate((r0, r1, r2, r3)):
        at = pl.multiple_of((t ^ k) * rows_of, rows_of)
        full[pl.ds(at, rows_of), :width] = nn(r[...], dbr_ref[...])
    line = lax.broadcasted_iota(jnp.int32, (128, width), 0)
    norms = jnp.where(
        line == 0,
        n1_ref[0:1, :],
        jnp.where(line == 1, n1_ref[1:2, :], jnp.where(line == 2, n2_ref[0:1, :], jnp.where(line == 3, n2_ref[1:2, :], 0.0))),
    )
    full[:, width:] = jnp.transpose(norms)
    rows = width // 8
    for block in range(8):
        k = d ^ block
        scr[(k & 1) * 4 + (k >> 1)] = full[block * rows : (block + 1) * rows, :].astype(jnp.bfloat16)
    even[...] = scr[0:4]
    odd[...] = scr[4:8]


def out_grad(scal, att, dbr, n1, n2):
    shard, width = dbr.shape
    rows, wide = width // 8, width + 128
    return pl.pallas_call(
        out_grad_kernel,
        out_shape=[sds((4, rows, wide))] * 2,
        in_specs=[SM] + [VM] * 7,
        out_specs=[VM] * 2,
        scratch_shapes=[pltpu.VMEM((width, wide), jnp.float32), pltpu.VMEM((8, rows, wide), jnp.bfloat16)],
        cost_estimate=cost(2 * shard * width * width, 6e6),
        name="out_grad",
    )(scal, *att, dbr, n1, n2)


def attend_back_kernel(heads, shard, scal, *refs):
    q_ref, k_ref, v_ref = refs[:3]
    o_refs, g_refs = refs[3:7], refs[7:11]
    lse_ref, cos_ref, sin_ref, segc_ref, segr_ref, mix_ref = refs[11:17]
    dm_ref = refs[17]
    parts = refs[18:22]
    dot_scr, don_scr, cen_scr, dq_scr, dk_scr, dv_scr = refs[22:]
    t = scal[0]
    per = shard // BLK
    for p in range(4):
        dot_scr[p] = g_refs[p][...]
        for h in range(heads):
            line = slice(64 * h, 64 * (h + 1))
            g = g_refs[p][line, :]
            prod = g.astype(jnp.float32) * o_refs[p][line, :].astype(jnp.float32)
            cen_scr[p, h : h + 1, :] = jnp.sum(prod, axis=0, keepdims=True)
            don_scr[h, p * shard : (p + 1) * shard, :] = jnp.transpose(g.astype(jnp.float32)).astype(jnp.bfloat16)
    dq_scr[...] = jnp.zeros_like(dq_scr)

    def place(b):
        return (b // per) ^ t, b % per

    def k_block(j, _):
        kp, khalf = place(j)
        k_row = pl.multiple_of(kp * shard + khalf * BLK, BLK)
        k_rows = pl.ds(k_row, BLK)
        seg_k = segc_ref[pl.ds(pl.multiple_of(j * BLK, BLK), BLK), :]
        for h in range(heads):
            dk_scr[h, k_rows, :] = jnp.zeros((BLK, 64), jnp.float32)
            dv_scr[h, k_rows, :] = jnp.zeros((BLK, 64), jnp.float32)

        def q_block(i, _):
            p, half = place(i)
            q_rows = pl.ds(pl.multiple_of(p * shard + half * BLK, BLK), BLK)
            lanes = pl.ds(pl.multiple_of(half * BLK, BLK), BLK)
            bias = jnp.where(seg_k == segr_ref[pl.ds(i, 1), :], 0.0, WORST)
            for h in range(heads):
                line = slice(64 * h, 64 * (h + 1))
                keys, q = k_ref[h, k_rows, :], q_ref[h, q_rows, :]
                s = nt(keys, q) + bias
                prob = jnp.exp(s - lse_ref[p, h : h + 1, lanes])
                dprob = nn(v_ref[h, k_rows, :], dot_scr[p, line, lanes])
                dscore = (prob * (dprob - cen_scr[p, h : h + 1, lanes])).astype(jnp.bfloat16)
                dv_scr[h, k_rows, :] += nn(prob.astype(jnp.bfloat16), don_scr[h, q_rows, :])
                dk_scr[h, k_rows, :] += nn(dscore, q)
                dq_scr[p, line, lanes] += tn(keys, dscore)
            return 0

        lax.fori_loop(scal[2 + j], scal[10 + j], q_block, 0)
        return 0

    lax.fori_loop(0, 4 * per, k_block, 0)
    for p in (3, 2, 1, 0):
        for half in range(per):
            lanes = slice(half * BLK, (half + 1) * BLK)
            rows = slice(p * shard + half * BLK, p * shard + (half + 1) * BLK)
            dq = jnp.transpose(dq_scr[p, :, lanes]) * 0.125
            at = pl.ds(pl.multiple_of((t ^ p) * shard + half * BLK, BLK), BLK)
            c, s = cos_ref[at, :], sin_ref[at, :]
            groups = [
                dq[:, :128],
                jnp.concatenate([dq[:, 128:], dk_scr[0, rows, :]], axis=1),
                jnp.concatenate([dk_scr[1, rows, :], dk_scr[2, rows, :]], axis=1),
            ]
            for n, z in enumerate(groups):
                dm_ref[rows, 128 * n : 128 * (n + 1)] = (z * c - swap_halves(z) * s).astype(jnp.bfloat16)
            dm_ref[rows, 384:512] = jnp.concatenate([dv_scr[0, rows, :], dv_scr[1, rows, :]], axis=1).astype(jnp.bfloat16)
            dm_ref[rows, 512:576] = dv_scr[2, rows, :].astype(jnp.bfloat16)
            parts[p][lanes, :] = nt(dm_ref[rows, :], mix_ref[...]).astype(jnp.bfloat16)


def attend_backward(scal, q, k, v, o, g, lse, cosine, sine, seg_col, seg_row, mix_full, heads):
    shard = o[0].shape[1]
    width, cols = mix_full.shape
    seq = 4 * shard
    return pl.pallas_call(
        functools.partial(attend_back_kernel, heads, shard),
        out_shape=[sds((seq, cols))] + [sds((shard, width))] * 4,
        in_specs=[SM] + [VM] * 17,
        out_specs=[VM] * 5,
        scratch_shapes=[
            pltpu.VMEM((4, heads * 64, shard), jnp.bfloat16),
            pltpu.VMEM((heads, seq, 64), jnp.bfloat16),
            pltpu.VMEM((4, 8, shard), jnp.float32),
            pltpu.VMEM((4, heads * 64, shard), jnp.float32),
            pltpu.VMEM((heads, seq, 64), jnp.float32),
            pltpu.VMEM((heads, seq, 64), jnp.float32),
        ],
        cost_estimate=cost(2 * seq * width * cols + 10 * 2 * seq * seq * 64 * heads, 25e6, seq * seq * heads / 2),
        name="attend_backward",
    )(scal, q, k, v, *o, *g, lse, cosine, sine, seg_col, seg_row, mix_full)


def mix_grad_kernel(scal, x0, x1, x2, x3, dm_ref, even, odd, scr):
    d = scal[1]
    shard, width = x0.shape
    grad = None
    for p, x in enumerate((x0, x1, x2, x3)):
        one = nn(jnp.transpose(x[...]), dm_ref[p * shard : (p + 1) * shard, :])
        grad = one if grad is None else grad + one
    rows = width // 8
    for block in range(8):
        k = d ^ block
        scr[(k & 1) * 4 + (k >> 1)] = grad[block * rows : (block + 1) * rows].astype(jnp.bfloat16)
    even[...] = scr[0:4]
    odd[...] = scr[4:8]


def mix_grad(scal, toks, dm):
    shard, width = toks[0].shape
    rows, cols = width // 8, dm.shape[1]
    return pl.pallas_call(
        mix_grad_kernel,
        out_shape=[sds((4, rows, cols))] * 2,
        in_specs=[SM] + [VM] * 5,
        out_specs=[VM] * 2,
        scratch_shapes=[pltpu.VMEM((8, rows, cols), jnp.bfloat16)],
        cost_estimate=cost(2 * 4 * shard * width * cols, 8e6),
        name="mix_grad",
    )(scal, *toks, dm)


def pt(a, k):
    return lax.ppermute(a, "tensor", [(s, s ^ k) for s in range(4)])


def pd(a, k):
    return lax.ppermute(a, "dp", [(s, s ^ k) for s in range(8)])


def by_owner(parts, t):
    low = (t & 1) == 1
    a, b, c, e = parts
    a, b, c, e = (jnp.where(low, b, a), jnp.where(low, a, b), jnp.where(low, e, c), jnp.where(low, c, e))
    high = (t & 2) == 2
    return (jnp.where(high, c, a), jnp.where(high, e, b), jnp.where(high, a, c), jnp.where(high, b, e))


def gather_dp(own):
    line = [own] + [pd(own, 2 * m) for m in (1, 2, 3)]
    side = [pd(a, 1) for a in line]
    return [piece for pair in zip(line, side) for piece in pair]


def gather_tensor(own):
    one, two = pt(own, 1), pt(own, 2)
    return [own, one, two, pt(two, 1)]


def wide_add(*parts):
    total = parts[0].astype(jnp.float32)
    for part in parts[1:]:
        total = total + part.astype(jnp.float32)
    return total


def scatter_tensor(parts):
    third = pt(parts[3], 1)
    one = pt(parts[1], 1)
    return parts[0], one, pt(wide_add(parts[2], third).astype(jnp.bfloat16), 2)


def scatter_dp(even, odd):
    got = pd(odd, 1)
    mine = [wide_add(even[m], got[m]) for m in range(4)]
    return wide_add(mine[0], *[pd(mine[m].astype(jnp.bfloat16), 2 * m) for m in (1, 2, 3)])


def row_tables(seg, head_dim):
    length = seg.shape[0]
    ids = jnp.arange(8, dtype=jnp.int32)
    begin = jnp.sum((seg[None, :] < ids[:, None]).astype(jnp.int32), axis=1)
    finish = jnp.sum((seg[None, :] <= ids[:, None]).astype(jnp.int32), axis=1)

    def pick(table, which):
        return jnp.sum(jnp.where(which[:, None] == ids[None, :], table[None, :], 0), axis=1)

    lo = pick(begin, seg[0::BLK]) // BLK
    hi = (pick(finish, seg[BLK - 1 :: BLK]) + BLK - 1) // BLK
    places = jnp.arange(length, dtype=jnp.int32) - pick(begin, seg)
    half = head_dim // 2
    freqs = rotary_base ** (-2.0 * jnp.arange(half, dtype=jnp.float32) / head_dim)
    angles = places.astype(jnp.float32)[:, None] * freqs
    c, s = jnp.cos(angles), jnp.sin(angles)
    return lo, hi, jnp.concatenate([c, c, c, c], axis=1), jnp.concatenate([-s, s, -s, s], axis=1)


def row_shards(
    tokens,
    cotangent,
    seg_ids,
    mix_weight,
    out_weight,
    gate_weight,
    up_weight,
    down_weight,
    first_gain,
    first_shift,
    second_gain,
    second_shift,
):
    t = lax.axis_index("tensor").astype(jnp.int32)
    d = lax.axis_index("dp").astype(jnp.int32)
    own = tokens[0]
    shard, width = own.shape
    heads = width // HEAD_DIM // 4
    mine = heads * HEAD_DIM
    few = mix_weight.shape[0]
    toks = gather_tensor(own)

    wide_out = jnp.concatenate(
        [
            out_weight,
            jnp.stack([first_gain, first_shift, second_gain, second_shift], axis=1),
            jnp.zeros((few, 124), jnp.bfloat16),
        ],
        axis=1,
    )
    by_part = mix_weight.reshape(few, 3, 4, mine)
    packs = []
    for k in range(4):
        columns = lax.dynamic_index_in_dim(by_part, t ^ k, axis=2, keepdims=False).reshape(few, 3 * mine)
        pack = jnp.concatenate([columns, wide_out], axis=1)
        packs.append(pack if k == 0 else pt(pack, k))
    rows = jnp.concatenate(by_owner(packs, t), axis=0)
    mix_parts = gather_dp(rows[:, : 3 * mine])
    out_parts = gather_dp(rows[:, 3 * mine :])
    ffn_parts = gather_dp(jnp.stack([gate_weight, up_weight, down_weight.T], axis=0))

    seg = seg_ids[0]
    lo, hi, cosine, sine = row_tables(seg, HEAD_DIM)
    scal = jnp.concatenate([jnp.stack([t, d]), lo, hi]).astype(jnp.int32)
    seg_col, seg_row = seg[:, None], seg.reshape(-1, BLK)

    res = attend(scal, mix_parts, toks, cosine, sine, seg_col, seg_row, heads)
    q, k, v, o, lse, mix_full = res[0], res[1], res[2], res[3:7], res[7], res[8]
    att = [o[0]] + [pt(o[p], p) for p in (1, 2, 3)]
    ffn_in, unit, inv, out_full, par = branch(scal, att, own, out_parts)
    weights = join(scal, ffn_parts)
    xs = gather_tensor(ffn_in)
    gate_a, up_a, hid_a, part0, part1 = ffn(xs[0], xs[1], weights)
    gate_b, up_b, hid_b, part2, part3 = ffn(xs[2], xs[3], weights)
    own_part, one, two = scatter_tensor([part0, part1, part2, part3])
    output, dsec, dlow, norm2 = second(own_part, one, two, unit, par, cotangent[0])
    ds = gather_tensor(dlow)
    dg_a, du_a, back0, back1 = ffn_back(ds[0], ds[1], gate_a, up_a, weights)
    dg_b, du_b, back2, back3 = ffn_back(ds[2], ds[3], gate_b, up_b, weights)
    own_back, one, two = scatter_tensor([back0, back1, back2, back3])
    ffn_even, ffn_odd = ffn_grad(scal, xs, ds, (hid_a, hid_b), (dg_a, dg_b), (du_a, du_b))
    ffn_sum = scatter_dp(ffn_even, ffn_odd)
    grads = first_back(scal, own_back, one, two, dsec, unit, inv, par, out_full)
    dfirst, dbr, das, norm1 = grads[0], grads[1], grads[2:6], grads[6]
    g = [das[0]] + [pt(das[p], p) for p in (1, 2, 3)]
    out_even, out_odd = out_grad(scal, att, dbr, norm1, norm2)
    out_sum = scatter_dp(out_even, out_odd)
    back = attend_backward(scal, q, k, v, o, g, lse, cosine, sine, seg_col, seg_row, mix_full, heads)
    dm, parts = back[0], back[1:5]
    own_tok, one, two = scatter_tensor(parts)
    grad_tokens = wide_add(dfirst, own_tok, one, two)
    mix_even, mix_odd = mix_grad(scal, toks, dm)
    mix_sum = scatter_dp(mix_even, mix_odd)

    out_low = out_sum.astype(jnp.bfloat16)
    pair = wide_add(out_sum, pt(out_low, 1))
    all_out = lax.dynamic_slice_in_dim(wide_add(pair, pt(pair.astype(jnp.bfloat16), 2)), t * few, few, 0)
    mix_rows = mix_sum.reshape(4, few, 3 * mine)
    pieces = []
    for j in range(4):
        piece = lax.dynamic_index_in_dim(mix_rows, t ^ j, axis=0, keepdims=False)
        pieces.append(piece if j == 0 else pt(piece.astype(jnp.bfloat16), j).astype(jnp.float32))
    columns = jnp.stack(by_owner(pieces, t), axis=1)
    grad_mix = columns.reshape(few, 4, 3, mine).transpose(0, 2, 1, 3).reshape(few, 12 * mine)
    return (
        output[None],
        grad_tokens[None],
        grad_mix,
        all_out[:, :width],
        ffn_sum[0],
        ffn_sum[1],
        ffn_sum[2].T,
        all_out[:, width],
        all_out[:, width + 1],
        all_out[:, width + 2],
        all_out[:, width + 3],
    )


def solution(mesh):
    in_specs = (
        P("dp", "tensor", None),
        P("dp", "tensor", None),
        P("dp", None),
        P(("dp", "tensor"), None),
        P(("dp", "tensor"), None),
        P("dp", "tensor"),
        P("dp", "tensor"),
        P("tensor", "dp"),
        P(("dp", "tensor")),
        P(("dp", "tensor")),
        P(("dp", "tensor")),
        P(("dp", "tensor")),
    )
    out_specs = (
        P("dp", "tensor", None),
        P("dp", "tensor", None),
        P(("dp", "tensor"), None),
        P(("dp", "tensor"), None),
        P("dp", "tensor"),
        P("dp", "tensor"),
        P("tensor", "dp"),
        P(("dp", "tensor")),
        P(("dp", "tensor")),
        P(("dp", "tensor")),
        P(("dp", "tensor")),
    )
    rows_fit = mesh.shape["tensor"] == 4 and mesh.shape["dp"] == 8
    body = row_shards if rows_fit else shards
    return jax.shard_map(body, mesh=mesh, in_specs=in_specs, out_specs=out_specs, check_vma=False)
```
